32 devices in a mesh: child: 2 (over core), rows: 16 (over z, y, x).
Axes of the slice: x: 2, y: 2, z: 4, core: 2. Of those that a mesh axis runs over, the one named last changes fastest.
Arguments:
- front_update: bfloat16 [2, 3072, 61440], P('child', 'rows'), may hold values from -0.0234375 to 0.0234375
- child_omega: bfloat16 [2, 61440, 256], P('child', 'rows'), may hold values from -6 to 6
- parent_block: bfloat16 [12288, 128], P(('child', 'rows')), may hold values from -0.5 to 0.5
- parent_omega: bfloat16 [12288, 256], P(('child', 'rows')), may hold values from -6 to 6
- child_map: int32 [2, 3072], replicated, may hold values from 0 to 12287, as said below
- leaf_order: int32 [12288], replicated, may hold values from 0 to 12287, as said below
Outputs:
- parent_samples: float32 [12288, 256], P(('child', 'rows'))
The draws below stay inside these ranges and needn't reach their ends.
Inputs may be any that keep to these rules, and one draw needn't show every extreme that they name: `child_map`: within one child the entries are distinct. Of each aligned block of 192 rows of one child, at most 12 entries fall in any one aligned block of 384 parent rows, and some block of parent rows gets exactly 12 from every such block. `leaf_order`: A permutation. Each aligned block of 384 leaf positions holds exactly 12 rows of every aligned block of 384 natural rows.
All inputs are finite; a program needn't handle non-finite values.
Results may differ from the reference program's by a relative error of at most 0.0003.
Values may be sent and summed in bfloat16 or wider, within the bound.
No kernel may reach another device: no remote copies, remote signals or barrier semaphores. Data moves between devices by JAX's collectives and lax.ppermute only.
A program may use at most 192 MiB of HBM per device.

```python
import jax
import jax.numpy as jnp
from jax import lax

ORDER = 61440
SAMPLES = 256
BLOCK = 128
ROWS_DEV = 192
OWNERS = 32
PARENT_DEV = 384
CHILD_ROWS = 3072
PARENT_ROWS = 12288
CAP = 12
LEAF_CAP = 12
N_CHILD = 2
N_ROWS = 16


def draw_child_map(key, part):
    base = jax.random.fold_in(key, 11)
    key_weight, key_forced, key_score, key_shuffle, key_local = jax.random.split(base, 5)
    slot_total = OWNERS * CAP
    slot_owner = jnp.arange(slot_total, dtype=jnp.int32) // CAP
    weights = jax.random.randint(key_weight, (OWNERS,), 1, 5)
    forced = jax.random.randint(key_forced, (), 0, OWNERS)
    raw_scores = jax.random.randint(key_score, (OWNERS, slot_total), 0, 262144)
    scores = raw_scores // weights[slot_owner][None, :]
    scores = jnp.where(slot_owner[None, :] == forced, -1, scores)
    scores = scores * slot_total + jnp.arange(slot_total, dtype=jnp.int32)[None, :]
    chosen = jnp.argsort(scores, axis=1, stable=True)[:, :ROWS_DEV]
    shuffle_keys = jax.random.randint(key_shuffle, (OWNERS, ROWS_DEV), 0, 65536) * ROWS_DEV + jnp.arange(ROWS_DEV, dtype=jnp.int32)[None, :]
    shuffle = jnp.argsort(shuffle_keys, axis=1, stable=True)
    chosen = jnp.take_along_axis(chosen, shuffle, axis=1)
    target_owner = (chosen // CAP).astype(jnp.int32).reshape(N_CHILD, N_ROWS * ROWS_DEV)
    one_hot = (target_owner[:, :, None] == jnp.arange(OWNERS, dtype=jnp.int32)[None, None, :]).astype(jnp.int32)
    arrival_rank = jnp.sum(one_hot * jnp.cumsum(one_hot, axis=1), axis=2) - 1
    local_keys = jax.random.randint(key_local, (N_CHILD, OWNERS, PARENT_DEV), 0, 65536) * PARENT_DEV + jnp.arange(PARENT_DEV, dtype=jnp.int32)[None, None, :]
    local_perm = jnp.argsort(local_keys, axis=2, stable=True).astype(jnp.int32)
    flat_index = (jnp.arange(N_CHILD, dtype=jnp.int32)[:, None] * OWNERS + target_owner) * PARENT_DEV + arrival_rank
    local_row = local_perm.reshape(-1)[flat_index]
    return (target_owner * PARENT_DEV + local_row).astype(jnp.int32)


def draw_leaf_order(key, part):
    base = jax.random.fold_in(key, 23)
    key_spread, key_place = jax.random.split(base, 2)
    counter = jnp.arange(PARENT_DEV, dtype=jnp.int32)[None, :]
    spread_keys = jax.random.randint(key_spread, (OWNERS, PARENT_DEV), 0, 65536) * PARENT_DEV + counter
    spread = jnp.argsort(spread_keys, axis=1, stable=True).astype(jnp.int32)
    place_keys = jax.random.randint(key_place, (OWNERS, PARENT_DEV), 0, 65536) * PARENT_DEV + counter
    place = jnp.argsort(place_keys, axis=1, stable=True).astype(jnp.int32)
    natural_owner = jnp.arange(OWNERS, dtype=jnp.int32)[:, None]
    leaf_owner = (natural_owner + spread % OWNERS) % OWNERS
    copy_index = spread // OWNERS
    leaf_local = place.reshape(-1)[leaf_owner * PARENT_DEV + LEAF_CAP * natural_owner + copy_index]
    leaf_position = leaf_owner * PARENT_DEV + leaf_local
    natural_row = natural_owner * PARENT_DEV + counter
    return jnp.zeros((PARENT_ROWS,), jnp.int32).at[leaf_position.reshape(-1)].set(natural_row.reshape(-1))


def steps_of(own_key, dims, pieces, low, largest):
    def one(position, shards_of):
        draws = jax.random.uniform(jax.random.fold_in(jax.random.fold_in(own_key, 6), position), (shards_of,), jnp.float32, low / len(pieces), largest / len(pieces))
        return jnp.repeat(jnp.exp(draws), dims[position] // shards_of).reshape((-1,) + (1,) * (len(dims) - position - 1))

    level = one(*pieces[0])
    for cut in pieces[1:]:
        level = level * one(*cut)
    return level


def centred(stream_key, shape, scale, bound, cuts=(), kind=jnp.bfloat16):
    result = jax.random.normal(stream_key, shape, jnp.float32) * scale
    if len(cuts) > 0:
        result = steps_of(stream_key, shape, cuts, -0.22, 0.18) * result
    return jnp.clip(result, min=-bound, max=bound).astype(kind)


def setup_inputs(seed: int = 0) -> dict:
    keys = jax.random.split(jax.random.key(seed), 7)
    return {
        "front_update": centred(keys[0], (N_CHILD, CHILD_ROWS, ORDER), ORDER ** -0.5, 0.0234375, ((0, 2), (1, 16))),
        "child_omega": centred(keys[1], (N_CHILD, ORDER, SAMPLES), 1.0, 6.0, ((0, 2), (1, 16))),
        "parent_block": centred(keys[2], (PARENT_ROWS, BLOCK), BLOCK ** -0.5, 0.5, ((0, 32),)),
        "parent_omega": centred(keys[3], (PARENT_ROWS, SAMPLES), 1.0, 6.0, ((0, 32),)),
        "child_map": draw_child_map(jax.random.fold_in(keys[6], 71), 0),
        "leaf_order": draw_leaf_order(jax.random.fold_in(keys[6], 71), 0),
    }


def reference(front_update, child_omega, parent_block, parent_omega, child_map, leaf_order):
    assembled = jnp.zeros((PARENT_ROWS, SAMPLES), jnp.float32)
    for front_id in range(N_CHILD):
        sampled = jnp.dot(front_update[front_id], child_omega[front_id], preferred_element_type=jnp.float32)
        assembled = assembled.at[child_map[front_id]].add(sampled)
    leaf_blocks = PARENT_ROWS // BLOCK
    own_samples = jnp.einsum(
        "bij,bjr->bir",
        parent_block.reshape(leaf_blocks, BLOCK, BLOCK).astype(jnp.float32),
        parent_omega.reshape(leaf_blocks, BLOCK, SAMPLES).astype(jnp.float32),
        precision=lax.Precision.HIGHEST,
    ).reshape(PARENT_ROWS, SAMPLES)
    assembled = assembled + own_samples
    return assembled[leaf_order]
```

```python
import functools

import jax
import jax.numpy as jnp
from jax import lax
from jax.experimental import pallas as pl
from jax.experimental.pallas import tpu as pltpu
from jax.sharding import PartitionSpec as P


PLAN = (
    (("XO", 1, 0, 0, 0), ("YO", 0, 1, 0, 0), ("XI", 1, 0, 1, 1), ("YI", 0, 1, 1, 1), ("PO", 0, 0, 1, 0), ("PI", 0, 0, 0, 0), ("C", 0, 0, 2, 0)),
    (("XO", 1, 0, 0, 1), ("YO", 0, 1, 0, 1), ("XI", 1, 0, 1, 0), ("YI", 0, 1, 1, 0), ("PO", 0, 0, 1, 1), ("PI", 0, 0, 0, 1), ("C", 0, 0, 3, 0)),
    (("XO", 1, 0, 1, 0), ("YO", 0, 1, 1, 0), ("XI", 1, 0, 2, 0), ("YI", 0, 1, 3, 0), ("PO", 0, 0, 2, 0), ("C", 0, 1, 2, 1)),
    (("XO", 1, 0, 1, 1), ("YO", 1, 1, 0, 0), ("XI", 1, 0, 0, 0), ("YI", 1, 1, 1, 0), ("PO", 0, 0, 3, 0), ("C", 0, 0, 3, 1)),
    (("XO", 1, 0, 2, 0), ("YO", 1, 1, 1, 0), ("XI", 1, 1, 3, 0), ("YI", 1, 1, 2, 0), ("PO", 0, 1, 2, 1), ("C", 0, 1, 2, 0)),
    (("XO", 1, 0, 3, 0), ("YO", 0, 1, 2, 0), ("XI", 1, 0, 3, 1), ("YI", 0, 1, 0, 0), ("PO", 0, 1, 3, 0), ("PI", 1, 1, 0, 0), ("C", 1, 0, 3, 0)),
    (("XO", 1, 1, 0, 1), ("YO", 1, 1, 1, 1), ("XI", 1, 1, 2, 1), ("YI", 1, 1, 3, 1), ("PO", 0, 0, 3, 1), ("C", 1, 0, 2, 1)),
    (("YO", 0, 0, 2, 1), ("YI", 0, 1, 0, 1), ("PO", 1, 0, 3, 1), ("C", 0, 0, 2, 1)),
    (("XO", 0, 1, 1, 1), ("YO", 0, 1, 3, 1), ("XI", 1, 1, 1, 1), ("YI", 0, 1, 3, 1), ("PO", 1, 0, 2, 1), ("PI", 1, 0, 0, 1), ("C", 1, 1, 0, 1)),
)
HANDED = (("PI", 1, 1, 2, 3), ("PI", 1, 1, 3, 4))


def grid_of(rows):
    power = rows.bit_length() - 1
    z_power = -(-power // 3)
    y_power = -(-(power - z_power) // 2)
    return 2**z_power, 2**y_power, 2 ** (power - z_power - y_power)


def bucket_rank(owner_ids, owners):
    one_hot = (owner_ids[:, None] == jnp.arange(owners, dtype=jnp.int32)[None, :]).astype(jnp.int32)
    running = jnp.cumsum(one_hot, axis=0)
    return jnp.sum(one_hot * running, axis=1) - 1


def select_rows(targets, total, values):
    picker = (targets[None, :] == jnp.arange(total, dtype=jnp.int32)[:, None]).astype(jnp.float32)
    return jnp.dot(
        picker, values, precision=lax.Precision.HIGHEST, preferred_element_type=jnp.float32
    )


def pick_rows(sources, values):
    picker = (sources[:, None] == jnp.arange(values.shape[0], dtype=jnp.int32)[None, :]).astype(
        jnp.float32
    )
    return jnp.dot(
        picker, values, precision=lax.Precision.HIGHEST, preferred_element_type=jnp.float32
    )


class Grid:
    def __init__(self, rows):
        self.z, self.y, self.x = grid_of(rows)
        self.rows = rows
        self.fits = (self.z, self.y, self.x) == (4, 2, 2)

    def place(self, r):
        return r // (self.y * self.x), (r // self.x) % self.y, r % self.x

    def index(self, z, y, x):
        return (z * self.y + y) * self.x + x

    def kind(self, r):
        return "I" if 0 < self.place(r)[0] < self.z - 1 else "O"

    def block(self, r, dx, dy, q):
        z, y, x = self.place(r)
        plane = q if z < self.z // 2 else self.z - 1 - q
        return self.index(plane, y ^ dy, x ^ dx)

    def pairs(self, link):
        found = []
        for r in range(self.rows):
            z, y, x = self.place(r)
            if link[0] == "C":
                if self.kind(r) == "I":
                    found.append((r, self.index(self.z - 1 - z, y, x)))
            elif link[0] == "P":
                if self.kind(r) != link[1]:
                    found.append((r, self.index(z ^ 1, y, x)))
            elif self.kind(r) == link[1]:
                found.append((r, r ^ 1 if link[0] == "X" else r ^ self.x))
        return found


SENDER = {"XO": "O", "YO": "O", "XI": "I", "YI": "I", "PO": "I", "PI": "O", "C": "I"}
TAKER = {"XO": "O", "YO": "O", "XI": "I", "YI": "I", "PO": "O", "PI": "I", "C": "I"}
BACK = {"PI": "PO", "XO": "XO", "XI": "XI"}


def across(link, item):
    dx, dy, q, *rest = item
    if link[0] == "X":
        dx ^= 1
    if link[0] == "Y":
        dy ^= 1
    if link[0] == "C":
        q = 3 - q
    return (dx, dy, q, *rest)


def multiply_kernel(
    units, n_slabs, n_blocks, chained, spot_ref, *refs
):
    slabs, refs = refs[:n_slabs], refs[n_slabs:]
    blocks, refs = refs[:n_blocks], refs[n_blocks:]
    if chained:
        before, refs = refs[0], refs[1:]
    total, left, right, sem = refs
    x, y, far, inner = (spot_ref[i] for i in range(4))
    kind_of = {"O": 0, "I": 1}
    counts = [sum(u[0] == k for u in units) for k in ("O", "I")]
    count = jnp.where(inner == 1, counts[1], counts[0])
    depth = right.shape[1]
    ordered = []
    seen = {"O": 0, "I": 0}
    for kind, *unit in units:
        ordered.append((kind_of[kind], seen[kind], *unit))
        seen[kind] += 1

    def start(number):
        slot = lax.rem(number, 2)
        for kind, place, slab, item, block, _ in ordered:
            @pl.when((inner == kind) & (number == place))
            def _():
                if item is None:
                    source = slabs[slab]
                else:
                    dx, dy, q = item
                    plane = jnp.where(far == 1, 3 - q, q)
                    index = plane * 4 + (y ^ dy) * 2 + (x ^ dx)
                    column = pl.multiple_of(index * depth, 128)
                    source = slabs[slab].at[:, pl.ds(column, depth)]
                pltpu.make_async_copy(source, left.at[slot], sem.at[0, slot]).start()
                pltpu.make_async_copy(blocks[block], right.at[slot], sem.at[1, slot]).start()

    total[...] = before[...] if chained else jnp.zeros_like(total)
    start(jnp.int32(0))

    def step(number, _):
        slot = lax.rem(number, 2)
        start(number + 1)
        pltpu.make_async_copy(blocks[0], right.at[slot], sem.at[1, slot]).wait()
        pltpu.make_async_copy(slabs[0].at[:, pl.ds(0, depth)], left.at[slot], sem.at[0, slot]).wait()
        half = jnp.int32(0)
        for kind, place, _, _, _, h in ordered:
            if h:
                half = jnp.where((inner == kind) & (number == place), h, half)
        total[half] += jnp.dot(left[slot], right[slot], preferred_element_type=jnp.float32)
        return 0

    lax.fori_loop(0, count, step, 0)


def multiply(spot, slabs, blocks, units, before=None):
    rows = slabs[0].shape[0]
    depth, width = blocks[0].shape
    hbm = pl.BlockSpec(memory_space=pltpu.HBM)
    vmem = pl.BlockSpec(memory_space=pltpu.VMEM)
    chained = before is not None
    specs = [pl.BlockSpec(memory_space=pltpu.SMEM)] + [hbm] * (len(slabs) + len(blocks))
    operands = [spot, *slabs, *blocks]
    if chained:
        specs.append(vmem)
        operands.append(before)
    return pl.pallas_call(
        functools.partial(multiply_kernel, units, len(slabs), len(blocks), chained),
        out_shape=jax.ShapeDtypeStruct((2, rows, width), jnp.float32),
        in_specs=specs,
        out_specs=vmem,
        scratch_shapes=[
            pltpu.VMEM((2, rows, depth), slabs[0].dtype),
            pltpu.VMEM((2, depth, width), blocks[0].dtype),
            pltpu.SemaphoreType.DMA((2, 2)),
        ],
        cost_estimate=pl.CostEstimate(
            flops=8 * rows * depth * width,
            bytes_accessed=8 * depth * (rows + width),
            transcendentals=0,
        ),
        compiler_params=pltpu.CompilerParams(vmem_limit_bytes=48 * 2**20),
    )(*operands)


def choose_kernel(count, spot_ref, *refs):
    outer, inner, out = refs[:count], refs[count : 2 * count], refs[2 * count : 3 * count]
    held, sem = refs[3 * count :]
    for number in range(count):
        for kind, source in ((0, outer), (1, inner)):
            @pl.when(spot_ref[3] == kind)
            def _():
                pltpu.make_async_copy(source[number], held.at[number], sem.at[0, number]).start()
    for number in range(count):
        pltpu.make_async_copy(outer[number], held.at[number], sem.at[0, number]).wait()
        pltpu.make_async_copy(held.at[number], out[number], sem.at[1, number]).start()
    for number in range(count):
        pltpu.make_async_copy(held.at[number], out[number], sem.at[1, number]).wait()


def choose(spot, outer, inner):
    count = len(outer)
    like = outer[0]
    hbm = pl.BlockSpec(memory_space=pltpu.HBM)
    return pl.pallas_call(
        functools.partial(choose_kernel, count),
        out_shape=[jax.ShapeDtypeStruct(like.shape, like.dtype)] * count,
        in_specs=[pl.BlockSpec(memory_space=pltpu.SMEM)] + [hbm] * (2 * count),
        out_specs=[hbm] * count,
        scratch_shapes=[
            pltpu.VMEM((count, *like.shape), like.dtype),
            pltpu.SemaphoreType.DMA((2, count)),
        ],
        compiler_params=pltpu.CompilerParams(vmem_limit_bytes=48 * 2**20),
    )(spot, *outer, *inner)


def sample_scheduled(slab, omega, row_id, grid):
    depth, cols = omega.shape
    half = cols // 2
    places = [grid.place(r) for r in range(grid.rows)]
    table = [[x, y, int(2 * z >= grid.z), int(0 < z < grid.z - 1)] for z, y, x in places]
    spot = jnp.asarray(table, dtype=jnp.int32)[row_id]
    x, y, far = spot[0], spot[1], spot[2]
    own = [omega[:, :half], omega[:, half:]]
    arrays = {
        "O": {(0, 0, 0, h): own[h] for h in (0, 1)},
        "I": {(0, 0, 1, h): own[h] for h in (0, 1)},
    }

    def columns(dx, dy, q):
        plane = jnp.where(far == 1, grid.z - 1 - q, q)
        index = (plane * grid.y + (y ^ dy)) * grid.x + (x ^ dx)
        return lax.dynamic_slice(slab, (0, index * depth), (slab.shape[0], depth))

    shipped = {}
    total = None
    probe = None
    finished = []
    last_first = max(t for t, sends in enumerate(PLAN, 1) if any(s[4] == 0 for s in sends))
    blocks = own[:]
    units = [(k, 0, (0, 0, q), h, h) for k, q in (("O", 0), ("I", 1)) for h in (0, 1)]
    for step, transfers in enumerate(PLAN, 1):
        for link, dx, dy, q, at in HANDED:
            if at == step:
                piece = columns(dx, dy, q)
                shipped[link, dx, dy, q] = lax.ppermute(piece, "rows", grid.pairs(link))
        families = {}
        for link, *item in transfers:
            families.setdefault(link[0], []).append((link, tuple(item)))
        operands = {}
        mixed = []
        for family, group in families.items():
            sources = {SENDER[l]: arrays[SENDER[l]][across(l, item)] for l, item in group}
            if len(set(id(a) for a in sources.values())) == 1:
                operands[family] = list(sources.values())[0]
            else:
                mixed.append((family, sources))
        if mixed:
            picked = choose(spot, [m[1]["O"] for m in mixed], [m[1]["I"] for m in mixed])
            operands.update({m[0]: value for m, value in zip(mixed, picked)})
        new = []
        for family, group in families.items():
            pairs = sorted(pair for link, _ in group for pair in grid.pairs(link))
            arrived = lax.ppermute(operands[family], "rows", pairs)
            probe = arrived if probe is None else probe
            for link, item in group:
                new.append((TAKER[link], item, arrived))
                units.append((TAKER[link], 0, item[:3], len(blocks), item[3]))
            blocks.append(arrived)
        for kind, item, arrived in new:
            arrays[kind][item] = arrived
        total = multiply(spot, [slab], blocks, units, total)
        blocks, units = [], []
        if step in (last_first, len(PLAN)):
            finished.append(total[len(finished)])
    for link in sorted(set(entry[0] for entry in HANDED)):
        for h in (0, 1):
            kind = TAKER[link]
            slabs, blocks, units = [], [], []
            for name, dx, dy, q, _ in HANDED:
                if name == link:
                    item = across(link, (dx, dy, q, h))
                    units.append((kind, len(slabs), None, len(blocks), 0))
                    slabs.append(shipped[link, dx, dy, q])
                    blocks.append(arrays[kind][item])
            term = multiply(spot, slabs, blocks, units)[0]
            finished[h] += lax.ppermute(term, "rows", grid.pairs(BACK[link]))
    return finished, probe


def body(front_update, child_omega, parent_block, parent_omega, child_map, leaf_order):
    children = lax.axis_size("child")
    row_count = lax.axis_size("rows")
    owners = children * row_count
    row_id = lax.axis_index("rows")
    device_id = lax.axis_index("child") * row_count + row_id
    slab = front_update[0]
    local_rows = slab.shape[0]
    sample_cols = child_omega.shape[2]
    grid = Grid(row_count)
    if grid.fits:
        pieces, probe = sample_scheduled(slab, child_omega[0], row_id, grid)
        child_map, leaf_order, parent_block, _ = lax.optimization_barrier(
            (child_map, leaf_order, parent_block, probe)
        )
    else:
        gathered = lax.all_gather(child_omega, "rows", axis=1, tiled=True)[0]
        pieces = [jnp.dot(slab, gathered, preferred_element_type=jnp.float32)]

    parent_dev = parent_block.shape[0]
    capacity = 2 * local_rows // owners
    route_table = child_map.reshape(owners, local_rows)
    my_targets = lax.dynamic_index_in_dim(route_table, device_id, 0, keepdims=False)
    target_owner = my_targets // parent_dev
    target_slot = target_owner * capacity + bucket_rank(target_owner, owners)

    arrives = route_table // parent_dev == device_id
    arrive_rank = jnp.cumsum(arrives.astype(jnp.int32), axis=1) - 1
    slot_column = jnp.where(arrives, arrive_rank, capacity)
    local_target = jnp.where(arrives, route_table % parent_dev - parent_dev, 0)
    in_slot = slot_column[:, None, :] == jnp.arange(capacity, dtype=jnp.int32)[None, :, None]
    places = parent_dev + jnp.sum(jnp.where(in_slot, local_target[:, None, :], 0), axis=2)
    places = places.reshape(-1)

    leaf_size = parent_block.shape[1]
    leaf_blocks = parent_dev // leaf_size
    own_samples = jnp.einsum(
        "bij,bjr->bir",
        parent_block.reshape(leaf_blocks, leaf_size, leaf_size),
        parent_omega.reshape(leaf_blocks, leaf_size, sample_cols),
        preferred_element_type=jnp.float32,
    ).reshape(parent_dev, sample_cols)

    parent_rows = leaf_order.shape[0]
    my_rows = device_id * parent_dev + jnp.arange(parent_dev, dtype=jnp.int32)
    is_mine = leaf_order[:, None] == my_rows[None, :]
    positions = jnp.arange(parent_rows, dtype=jnp.int32)[:, None]
    my_positions = jnp.sum(jnp.where(is_mine, positions, 0), axis=0)
    leaf_owner = my_positions // parent_dev
    leaf_capacity = parent_dev // owners
    leaf_slot = leaf_owner * leaf_capacity + bucket_rank(leaf_owner, owners)

    natural = lax.dynamic_slice_in_dim(leaf_order, device_id * parent_dev, parent_dev)
    anchor = natural // parent_dev
    offset = natural % parent_dev
    same_anchor = anchor[:, None] == anchor[None, :]
    earlier = offset[None, :] < offset[:, None]
    arrival_rank = jnp.sum((same_anchor & earlier).astype(jnp.int32), axis=1)
    leaf_source = anchor * leaf_capacity + arrival_rank

    def exchange(values, rows_each):
        width = values.shape[1]
        return lax.all_to_all(
            values.reshape(owners, rows_each, width),
            ("child", "rows"),
            split_axis=0,
            concat_axis=0,
            tiled=True,
        ).reshape(owners * rows_each, width)

    outputs = []
    start = 0
    for sampled in pieces:
        width = sampled.shape[1]
        outgoing = select_rows(target_slot, owners * capacity, sampled)
        incoming = exchange(outgoing, capacity)
        assembled = select_rows(places, parent_dev, incoming)
        assembled = assembled + own_samples[:, start : start + width]
        arrived = exchange(select_rows(leaf_slot, owners * leaf_capacity, assembled), leaf_capacity)
        outputs.append(pick_rows(leaf_source, arrived))
        start += width
    return outputs[0] if len(outputs) == 1 else jnp.concatenate(outputs, axis=1)


def solution(mesh):
    placed = (
        P("child", "rows", None),
        P("child", "rows", None),
        P(("child", "rows"), None),
        P(("child", "rows"), None),
        P(),
        P(),
    )
    step = jax.shard_map(
        body, mesh=mesh, in_specs=placed, out_specs=P(("child", "rows"), None), check_vma=False
    )
    if not Grid(mesh.shape["rows"]).fits:
        return step
    return step
```
